32 devices in a mesh: gx: 4 (over x, core), gy: 8 (over z, y).
Axes of the slice: x: 2, y: 2, z: 4, core: 2. Of those that a mesh axis runs over, the one named last changes fastest.
Arguments:
- blocks: float32 [8, 8, 9, 128, 128], P('gx', 'gy'), may hold values from -0.0625 to 0.0625
- pair_mask: int32 [8, 8, 9, 8, 8], P('gx', 'gy'), may hold values 0 or 1
- rhs_rows: float32 [8, 8, 9, 128, 128], P('gx', 'gy'), may hold values from -6 to 6
- counts: int32 [8, 8, 8], P('gx', 'gy'), may hold values from 1 to 3, as said below
Outputs:
- solution: float32 [8, 8, 9, 128, 128], P('gx', 'gy')
The draws below stay inside these ranges and needn't reach their ends.
Inputs may be any that keep to these rules, and one draw needn't show every extreme that they name: `counts`: cut the first block index into runs of 2 blocks. Within each second index b, run a and run a + 2 together hold at most 2 blocks that have an atom with a count of 2 or more, and some run holds 2 such blocks; at least one atom takes 3 iterations and at least one takes 1.
All inputs are finite; a program needn't handle non-finite values. No bound on the sum of `pair_mask` on one device may be relied on, other than what follows from the above.
Results may differ from the reference program's by a relative error of at most 0.0003.
Values sent between devices are 32-bit elements; how exact they have to be, the bound alone decides.
A program may use at most 128 MiB of HBM per device.

```python
import jax
import jax.numpy as jnp
from jax import lax

ORB = 16
ATOMS = 8
B = 128
OFFSETS = 9
GRP_X = 2
ITERS = 3
NGX = 8
NGY = 8


def draw_counts(key, part):
    groups = NGX // GRP_X
    half_groups = groups // 2
    pair_count = half_groups * NGY
    key_total = jax.random.fold_in(key, 21)
    key_split = jax.random.fold_in(key, 22)
    key_forced = jax.random.fold_in(key, 23)
    key_scores = jax.random.fold_in(key, 24)
    key_base = jax.random.fold_in(key, 25)
    key_leading = jax.random.fold_in(key, 26)
    key_lead_val = jax.random.fold_in(key, 27)
    totals = jax.random.randint(key_total, (pair_count,), 0, GRP_X + 1, dtype=jnp.int32)
    lower = jax.random.randint(key_split, (pair_count,), 0, totals + 1, dtype=jnp.int32)
    forced = jax.random.randint(key_forced, (), 0, pair_count, dtype=jnp.int32)
    pair_ids = jnp.arange(pair_count, dtype=jnp.int32)
    totals = jnp.where(pair_ids == forced, GRP_X, totals)
    lower = jnp.where(pair_ids == forced, GRP_X, lower)
    upper = totals - lower
    loads = jnp.concatenate([lower.reshape(half_groups, NGY), upper.reshape(half_groups, NGY)], axis=0)
    local_ids = jnp.arange(GRP_X, dtype=jnp.int32)
    scores = jax.random.randint(key_scores, (groups, NGY, GRP_X), 0, 1 << 20, dtype=jnp.int32) * GRP_X + local_ids
    ranks = jnp.argsort(jnp.argsort(scores, axis=-1), axis=-1).astype(jnp.int32)
    slow = ranks < loads[..., None]
    base_counts = jax.random.randint(key_base, (groups, NGY, GRP_X, ATOMS), 1, 4, dtype=jnp.int32)
    leading = jax.random.randint(key_leading, (groups, NGY, GRP_X), 0, ATOMS, dtype=jnp.int32)
    lead_val = jax.random.randint(key_lead_val, (groups, NGY, GRP_X), 2, 4, dtype=jnp.int32)
    group_ids = jnp.arange(groups, dtype=jnp.int32)[:, None, None]
    column_ids = jnp.arange(NGY, dtype=jnp.int32)[None, :, None]
    forced_device = (group_ids == forced // NGY) & (column_ids == forced % NGY) & (ranks == 0)
    lead_val = jnp.where(forced_device, ITERS, lead_val)
    atom_ids = jnp.arange(ATOMS, dtype=jnp.int32)
    atom_counts = jnp.where(atom_ids == leading[..., None], lead_val[..., None], base_counts)
    result = jnp.where(slow[..., None], atom_counts, 1)
    result = jnp.transpose(result, (0, 2, 1, 3)).reshape(NGX, NGY, ATOMS)
    return result.astype(jnp.int32)


def touch_ends(values, rng, least, largest):
    spot = [jax.random.randint(jax.random.fold_in(rng, axis), (), 0, length) for axis, length in enumerate(values.shape)]
    widest = values.shape.index(max(values.shape))
    neighbour = spot[:widest] + [(spot[widest] + 1) % values.shape[widest]] + spot[widest + 1:]
    return values.at[tuple(spot)].set(least).at[tuple(neighbour)].set(largest)


def steps_of(rng, shape, split, low, top_value):
    gain, own = 1.0, jax.random.fold_in(rng, 6)
    for dim, parts in split:
        draws = jnp.exp(jax.random.uniform(jax.random.fold_in(own, dim), (parts,), jnp.float32, low / len(split), top_value / len(split)))
        gain = gain * jnp.repeat(draws, shape[dim] // parts).reshape([-1 if axis == dim else 1 for axis in range(len(shape))])
    return gain


def normal_values(own_key, extent, deviation, bound, cuts=(), held_as=jnp.bfloat16):
    array = jax.random.normal(own_key, extent, jnp.float32) * deviation
    if len(cuts) > 0:
        array = steps_of(own_key, extent, cuts, -0.22, 0.18) * array
    return jnp.clip(array, min=-bound, max=bound).astype(held_as)


def setup_inputs(seed: int = 0) -> dict:
    seeds = jax.random.split(jax.random.key(seed), 5)
    blocks = normal_values(seeds[0], (NGX, NGY, OFFSETS, B, B), (81 * B) ** -0.5, 0.0625, ((0, 4), (1, 8)), jnp.float32)
    pair_mask = touch_ends((jax.random.randint(seeds[1], (NGX, NGY, OFFSETS, ATOMS, ATOMS), 0, 4) < 3).astype(jnp.int32), jax.random.fold_in(seeds[1], 1), 0, 1)
    rhs_rows = normal_values(seeds[2], (NGX, NGY, OFFSETS, B, B), 1.0, 6.0, ((0, 4), (1, 8)), jnp.float32)
    counts = draw_counts(jax.random.fold_in(seeds[4], 71), 0)
    return dict(blocks=blocks, pair_mask=pair_mask, rhs_rows=rhs_rows, counts=counts)


def expand_mask(pair_mask, orbitals):
    shaped = pair_mask.astype(jnp.float32)[..., :, None, :, None]
    leading = pair_mask.shape[:-2]
    atom_count = pair_mask.shape[-1]
    expanded = jnp.broadcast_to(shaped, leading + (atom_count, orbitals, atom_count, orbitals))
    return expanded.reshape(leading + (atom_count * orbitals, atom_count * orbitals))

def cluster_apply(window, vectors):
    result = vectors
    for row_off in (-1, 0, 1):
        for col_off in (-1, 0, 1):
            offset = 3 * (row_off + 1) + (col_off + 1)
            row_low, row_high = (max(0, -row_off), min(3, 3 - row_off))
            col_low, col_high = (max(0, -col_off), min(3, 3 - col_off))
            coupled = window[..., row_low:row_high, col_low:col_high, offset, :, :]
            source = vectors[..., row_low + row_off:row_high + row_off, col_low + col_off:col_high + col_off, :, :]
            product = jnp.einsum('...xyij,...xyjc->...xyic', coupled, source, precision=lax.Precision.HIGHEST)
            result = result.at[..., row_low:row_high, col_low:col_high, :, :].add(-product)
    return result

def cluster_rhs(rhs_window):
    rows_list = []
    for row_pos in range(3):
        pieces = []
        for col_pos in range(3):
            pieces.append(rhs_window[..., row_pos, col_pos, 8 - 3 * row_pos - col_pos, :, :])
        rows_list.append(jnp.stack(pieces, axis=-3))
    return jnp.stack(rows_list, axis=-4)

def column_inner(left, other):
    return lax.optimization_barrier(jnp.sum(left * other, axis=(-4, -3, -2)))

def spread(scalar):
    return scalar[..., None, None, None, :]

def guarded(top, bottom, floor_val):
    return top * bottom / (bottom * bottom + floor_val * floor_val)

def start_state(window, right_side):
    image_first = cluster_apply(window, right_side)
    zero_field = jnp.zeros_like(right_side)
    norm_rhs = column_inner(right_side, right_side)
    zero_cols = jnp.zeros_like(norm_rhs)
    vectors = (right_side, right_side, right_side, image_first, image_first, zero_field, zero_field)
    scalars = (norm_rhs, 0.1 * norm_rhs, jnp.sqrt(norm_rhs), zero_cols, zero_cols, norm_rhs)
    return (vectors, scalars)

def iterate(window, vectors, scalars, iteration, limit_cols):
    shadow, residual, first_dir, image_first, vector, direction, solution = vectors
    rho_value, rho_floor, tau_value, theta_value, eta_value, norm_rhs = scalars
    alpha_floor = 0.1 * jnp.sqrt(norm_rhs * (column_inner(vector, vector) + 1e-06))
    alpha_value = guarded(rho_value, column_inner(shadow, vector), alpha_floor)
    step_ratio = guarded(1.0, alpha_value, 0.1)
    second = first_dir - spread(alpha_value) * vector
    image_second = cluster_apply(window, second)
    active = spread((limit_cols > iteration).astype(jnp.float32))
    for half_dir, half_image in ((first_dir, image_first), (second, image_second)):
        residual = residual - spread(alpha_value) * half_image
        direction = half_dir + spread(theta_value * theta_value * eta_value * step_ratio) * direction
        theta_value = jnp.sqrt(column_inner(residual, residual)) / tau_value
        cosine = 1.0 / jnp.sqrt(1.0 + theta_value * theta_value)
        tau_value = tau_value * theta_value * cosine
        eta_value = cosine * cosine * alpha_value
        solution = solution + active * spread(eta_value) * direction
    vectors = (shadow, residual, second, image_second, vector, direction, solution)
    scalars = (rho_value, rho_floor, tau_value, theta_value, eta_value, norm_rhs)
    return (vectors, scalars)

def advance(window, vectors, scalars):
    shadow, residual, second, image_second, vector, direction, solution = vectors
    rho_value, rho_floor, tau_value, theta_value, eta_value, norm_rhs = scalars
    rho_next = column_inner(shadow, residual)
    beta_value = guarded(rho_next, rho_value, rho_floor)
    next_floor = 0.1 * jnp.sqrt(norm_rhs * column_inner(residual, residual))
    first_dir = residual + spread(beta_value) * second
    image_first = cluster_apply(window, first_dir)
    vector = image_first + spread(beta_value) * (image_second + spread(beta_value) * vector)
    vectors = (shadow, residual, first_dir, image_first, vector, direction, solution)
    scalars = (rho_next, next_floor, tau_value, theta_value, eta_value, norm_rhs)
    return (vectors, scalars)

def first_section(window, right_side, limit_cols):
    vectors, scalars = start_state(window, right_side)
    return iterate(window, vectors, scalars, 0, limit_cols)

def later_section(window, vectors, scalars, limit_cols):
    for iteration in range(1, ITERS):
        vectors, scalars = advance(window, vectors, scalars)
        vectors, scalars = iterate(window, vectors, scalars, iteration, limit_cols)
    return vectors[6]

def reference(blocks, pair_mask, rhs_rows, counts):
    coupling = blocks * expand_mask(pair_mask, ORB)
    widths = ((1, 1), (1, 1), (0, 0), (0, 0), (0, 0))
    padded_coupling = jnp.pad(coupling, widths)
    padded_rhs = jnp.pad(rhs_rows, widths)
    limits = jnp.repeat(counts, ORB, axis=-1).astype(jnp.float32)

    def one_group(block_index):
        zero_idx = jnp.zeros((), jnp.int32)
        first_pos = (block_index // NGY).astype(jnp.int32)
        second_pos = (block_index % NGY).astype(jnp.int32)
        starts = (first_pos, second_pos, zero_idx, zero_idx, zero_idx)
        window = lax.dynamic_slice(padded_coupling, starts, (3, 3, OFFSETS, B, B))
        rhs_window = lax.dynamic_slice(padded_rhs, starts, (3, 3, OFFSETS, B, B))
        limit_cols = lax.dynamic_slice(limits, (first_pos, second_pos, zero_idx), (1, 1, B)).reshape(B)
        vectors, scalars = first_section(window, cluster_rhs(rhs_window), limit_cols)
        return later_section(window, vectors, scalars, limit_cols)
    result = lax.map(one_group, jnp.arange(NGX * NGY, dtype=jnp.int32))
    return result.reshape(NGX, NGY, OFFSETS, B, B)
```

```python
import functools

import jax
import jax.numpy as jnp
from jax import lax
from jax.experimental import pallas as pl
from jax.experimental.pallas import tpu as pltpu
from jax.sharding import PartitionSpec as P

ITERS = 3
MESH = pl.DeviceIdType.MESH
F32 = jnp.float32
BF16 = jnp.bfloat16
CHUNK = 64


def guarded(top, bottom, floor_val):
    return top * bottom / (bottom * bottom + floor_val * floor_val)


def split(value):
    high = value.astype(BF16)
    return high, (value - high.astype(F32)).astype(BF16)


def kernel(
    blocks, masks, rhs, limits, out,
    own_c, gy_c, gx_c, dg_c, gy_m, gx_m, dg_m, gy_r,
    mid, edge, v_hi, v_lo, res,
    shadow, w_vec, y_first, y_second, u_first, u_second, vec, direc, sol,
    send_sem, recv_sem, local_sem,
):
    b = blocks.shape[-1]
    orb = b // masks.shape[-2]
    strip = 3 * b
    rows = 9 * b
    gx, gy = lax.axis_index("gx"), lax.axis_index("gy")
    ngx, ngy = lax.axis_size("gx"), lax.axis_size("gy")
    gx_to = (gx < ngx - 1, gx > 0)
    gx_from = (gx > 0, gx < ngx - 1)
    gy_to = (gy < ngy - 1, gy > 0)
    gy_from = (gy > 0, gy < ngy - 1)
    gx_dev = ((gx + 1, gy), (gx - 1, gy))
    gy_dev = ((gx, gy + 1), (gx, gy - 1))

    def place(ref, group, row_off, col_off):
        return ref.at[
            pl.ds(strip * (row_off + 1) + b * (col_off + 1), b), pl.ds(b * group, b)
        ]

    count = [0]

    def remote(src, dst, device):
        number = count[0]
        count[0] += 1
        return pltpu.make_async_remote_copy(
            src_ref=src, dst_ref=dst, send_sem=send_sem.at[number],
            recv_sem=recv_sem.at[number], device_id=device, device_id_type=MESH,
        )

    row_of = (1, 0)
    ou_of = (1, 0)
    ov_of = (1, 0)
    far = (2, 0)
    pairs = ((0, 0, 1, 0), (0, 1, 2, -1), (1, 0, 0, 1), (1, 1, 1, 0))

    gy_early, gy_late, gx_direct, diag = {}, {}, {}, {}
    for t in (0, 1):
        early, late = [], []
        ov = far[t]
        early.append(remote(
            masks.at[:, :, pl.ds(ov_of[t], 2)], gy_m.at[t], gy_dev[t]))
        for s in (0, 1):
            early.append(remote(
                rhs.at[row_of[s], far[s], ov], gy_r.at[t, s], gy_dev[t]))
        for s in (0, 1):
            early.append(remote(
                blocks.at[row_of[s], pl.ds(ou_of[s], 2), pl.ds(ov_of[t], 2)],
                gy_c.at[t, row_of[s], pl.ds(ou_of[s], 2)], gy_dev[t]))
        for row, group, ou, row_off in pairs:
            late.append(remote(
                rhs.at[row, ou, ov], place(shadow, group, row_off, 2 * t - 1), gy_dev[t]))
        for s in (0, 1):
            ou = 2 - far[s]
            late.append(remote(
                blocks.at[row_of[s], ou, pl.ds(ov_of[t], 2)],
                gy_c.at[t, row_of[s], ou], gy_dev[t]))
        gy_early[t], gy_late[t] = early, late
    for s in (0, 1):
        row_off = 2 * s - 1
        gx_direct[s] = [
            remote(rhs.at[row_of[s], far[s], 1], place(shadow, s, row_off, 0), gx_dev[s]),
            remote(masks.at[row_of[s], pl.ds(ou_of[s], 2)], gx_m.at[s], gx_dev[s]),
            remote(blocks.at[row_of[s], pl.ds(ou_of[s], 2)], gx_c.at[s], gx_dev[s]),
        ]
        for t in (0, 1):
            diag[s, t] = [
                remote(gy_r.at[t, s], place(shadow, s, row_off, 2 * t - 1), gx_dev[s]),
                remote(gy_m.at[t, row_of[s], pl.ds(ou_of[s], 2)], dg_m.at[s, t], gx_dev[s]),
                remote(gy_c.at[t, row_of[s], pl.ds(ou_of[s], 2)], dg_c.at[s, t], gx_dev[s]),
            ]

    barrier = pltpu.get_barrier_semaphore()
    total = jnp.int32(0)
    for exists, device in zip(gx_to + gy_to, gx_dev + gy_dev):
        total = total + exists.astype(jnp.int32)

        @pl.when(exists)
        def _(device=device):
            pl.semaphore_signal(barrier, inc=1, device_id=device, device_id_type=MESH)
    pl.semaphore_wait(barrier, total)

    def start(condition, copies):
        @pl.when(condition)
        def _():
            for copy in copies:
                copy.start()

    for t in (0, 1):
        start(gy_to[t], gy_early[t])
    for s in (0, 1):
        start(gx_to[s], gx_direct[s])
    for t in (0, 1):
        start(gy_to[t], gy_late[t])

    locals_ = [pltpu.make_async_copy(blocks, own_c, local_sem.at[0])]
    for number, (row, group, ou, row_off) in enumerate(pairs):
        locals_.append(pltpu.make_async_copy(
            rhs.at[row, ou, 1], place(shadow, group, row_off, 0), local_sem.at[1 + number]))
    for copy in locals_:
        copy.start()

    def clear(ref):
        ref[...] = jnp.zeros(ref.shape, ref.dtype)

    def clear_rows(ref):
        def body(index, _):
            ref[pl.ds(index * b, b), :] = jnp.zeros((b, ref.shape[1]), ref.dtype)
            return 0
        lax.fori_loop(0, ref.shape[0] // b, body, 0)

    for ref in (u_second, vec, direc, sol):
        clear_rows(ref)
    clear_rows(v_hi)
    clear_rows(v_lo)
    zero = jnp.zeros((b, b), BF16)
    for ref in (mid, edge):
        for which in (0, 1):
            for part in (0, 1):
                for near in range(ref.shape[-1] // strip):
                    ref[which, part, 0:b, strip * near + 2 * b:strip * near + 3 * b] = zero
                    ref[which, part, 2 * b:3 * b, strip * near:strip * near + b] = zero

    def put(w, c, ou, ov, value, mask):
        masked = (value.reshape(b // orb, orb, b) * mask[:, None, :]).reshape(b, b)
        high, low = split(masked)
        base = (0, 0, 1, 2)[w]
        ref, which = ((edge, 0), (mid, 0), (mid, 1), (edge, 1))[w]
        col = strip * (w + ou - 1 - base) + b * (c + ov - 1)
        ref[which, 0, b * c:b * (c + 1), col:col + b] = high
        ref[which, 1, b * c:b * (c + 1), col:col + b] = low

    def finish(condition, copies, otherwise):
        @pl.when(condition)
        def _():
            for copy in copies:
                copy.wait_recv()

        @pl.when(jnp.logical_not(condition))
        def _():
            for ref in otherwise:
                clear(ref)

    locals_[0].wait()
    own_masks = limits[1]
    for row in (0, 1):
        for ou in range(3):
            for ov in range(3):
                put(row + 1, 1, ou, ov, own_c[row, ou, ov], own_masks[row, ou, ov])

    for t in (0, 1):
        @pl.when(gy_from[t])
        def _(t=t):
            for copy in gy_early[t]:
                copy.wait_recv()
        for s in (0, 1):
            start(jnp.logical_and(gy_from[t], gx_to[s]), diag[s, t])

    for s in (0, 1):
        finish(gx_from[s], gx_direct[s],
               [place(shadow, s, 2 * s - 1, 0), gx_m.at[s], gx_c.at[s]])
        for ou in range(2):
            for ov in range(3):
                put(3 * s, 1, ou + ou_of[s], ov, gx_c[s, ou, ov], gx_m[s, ou, ov])

    for t in (0, 1):
        @pl.when(jnp.logical_not(gy_from[t]))
        def _(t=t):
            clear(gy_m.at[t])
            for s in (0, 1):
                for ou in range(2):
                    for ov in range(2):
                        clear(gy_c.at[t, row_of[s], ou + ou_of[s], ov])
        for s in (0, 1):
            for ou in range(2):
                for ov in range(2):
                    at = (t, row_of[s], ou + ou_of[s], ov)
                    put(row_of[s] + 1, 2 * t, at[2], ov + ov_of[t], gy_c[at], gy_m[at])
    for t in (0, 1):
        for s in (0, 1):
            finish(jnp.logical_and(gx_from[s], gy_from[t]), diag[s, t],
                   [place(shadow, s, 2 * s - 1, 2 * t - 1), dg_m.at[s, t], dg_c.at[s, t]])
            for ou in range(2):
                for ov in range(2):
                    put(3 * s, 2 * t, ou + ou_of[s], ov + ov_of[t],
                        dg_c[s, t, ou, ov], dg_m[s, t, ou, ov])
    for copy in locals_[1:]:
        copy.wait()
    for t in (0, 1):
        finish(gy_from[t], gy_late[t],
               [place(shadow, group, row_off, 2 * t - 1) for _, group, _, row_off in pairs]
               + [gy_c.at[t, row_of[s], 2 - far[s]] for s in (0, 1)])
        for s in (0, 1):
            for ov in range(2):
                at = (t, row_of[s], 2 - far[s], ov)
                put(row_of[s] + 1, 2 * t, at[2], ov + ov_of[t], gy_c[at], gy_m[at])

    def over_chunks(body, sums):
        def step(index, carry):
            return body(pl.ds(pl.multiple_of(index * CHUNK, CHUNK), CHUNK), index * CHUNK, carry)
        return lax.fori_loop(
            0, rows // CHUNK, step, tuple(jnp.zeros((8, 2 * b), F32) for _ in range(sums)))

    def fold(value):
        return jnp.sum(value.reshape(CHUNK // 8, 8, 2 * b), axis=0)

    def column(value):
        return jnp.sum(value, axis=0, keepdims=True)

    def store_split(first, value):
        high, low = split(value)
        for ref, part in ((v_hi, high), (v_lo, low)):
            ref[pl.ds(pl.multiple_of(first, CHUNK), CHUNK), 0:b] = part[:, 0:b]
            ref[pl.ds(pl.multiple_of(first + strip, CHUNK), CHUNK), b:2 * b] = part[:, b:]

    def product(left, right):
        return jnp.dot(left, right, preferred_element_type=F32)

    def apply():
        for w in range(4):
            if w in (0, 3):
                which = w // 3
                near = pl.ds(2 * strip * which, 2 * strip)
                cols = slice(b * which, b * (which + 1))
                high, low = edge[which, 0], edge[which, 1]
            else:
                near = pl.ds(strip * (w - 1), 3 * strip)
                cols = slice(0, 2 * b)
                high, low = mid[w - 1, 0], mid[w - 1, 1]
            v_high, v_low = v_hi[near, cols], v_lo[near, cols]
            value = product(high, v_high) + product(low, v_high) + product(high, v_low)
            if w < 3:
                res[strip * w:strip * (w + 1), 0:b] = value[:, 0:b]
            if w > 0:
                res[strip * (w - 1):strip * w, b:2 * b] = value[:, -b:]

    def prepare(at, first, sums):
        value = shadow[at, :]
        w_vec[at, :] = value
        y_first[at, :] = value
        store_split(first, value)
        return (sums[0] + fold(value * value),)

    norm = column(over_chunks(prepare, 1)[0])
    limit = limits[0][...]

    def iteration(index, carry):
        rho, beta, tau, theta, eta, ratio = carry
        active = (limit > index.astype(F32)).astype(F32)
        apply()

        def after_first(at, first, sums):
            image = y_first[at, :] - res[at, :]
            u_first[at, :] = image
            value = image + beta * (u_second[at, :] + beta * vec[at, :])
            vec[at, :] = value
            return sums[0] + fold(value * value), sums[1] + fold(shadow[at, :] * value)

        square, along = (column(v) for v in over_chunks(after_first, 2))
        alpha = guarded(rho, along, 0.1 * jnp.sqrt(norm * (square + 1e-06)))
        ratio = guarded(1.0, alpha, 0.1)
        keep = theta * theta * eta * ratio

        def between(at, first, sums):
            y_one = y_first[at, :]
            residual = w_vec[at, :] - alpha * u_first[at, :]
            w_vec[at, :] = residual
            direc[at, :] = y_one + keep * direc[at, :]
            second = y_one - alpha * vec[at, :]
            y_second[at, :] = second
            store_split(first, second)
            return (sums[0] + fold(residual * residual),)

        size = column(over_chunks(between, 1)[0])

        def turn(size, tau):
            theta = jnp.sqrt(size) / tau
            cosine = 1.0 / jnp.sqrt(1.0 + theta * theta)
            return theta, tau * theta * cosine, cosine * cosine * alpha

        theta, tau, eta = turn(size, tau)
        eta_one = active * eta
        apply()

        def after_second(at, first, sums):
            image = y_second[at, :] - res[at, :]
            u_second[at, :] = image
            residual = w_vec[at, :] - alpha * image
            w_vec[at, :] = residual
            return sums[0] + fold(residual * residual), sums[1] + fold(shadow[at, :] * residual)

        size, rho_next = (column(v) for v in over_chunks(after_second, 2))
        keep = theta * theta * eta * ratio
        theta, tau, eta = turn(size, tau)
        eta_two = active * eta
        return keep, eta_one, eta_two, rho_next, size, tau, theta, eta, ratio

    def close(beta, keep, eta_one, eta_two):
        def body(at, first, sums):
            one, second = direc[at, :], y_second[at, :]
            two = second + keep * one
            direc[at, :] = two
            sol[at, :] = sol[at, :] + eta_one * one + eta_two * two
            value = w_vec[at, :] + beta * second
            y_first[at, :] = value
            store_split(first, value)
            return sums
        over_chunks(body, 0)

    zero_row = jnp.zeros_like(norm)

    def whole(index, carry):
        rho, floor, beta, tau, theta, eta, ratio = carry
        keep, eta_one, eta_two, rho_next, size, tau, theta, eta, ratio = iteration(
            index, (rho, beta, tau, theta, eta, ratio))
        beta = guarded(rho_next, rho, floor)
        floor = 0.1 * jnp.sqrt(norm * size)
        close(beta, keep, eta_one, eta_two)
        return rho_next, floor, beta, tau, theta, eta, ratio

    lax.fori_loop(0, ITERS, whole, (
        norm, 0.1 * norm, zero_row, jnp.sqrt(norm), zero_row, zero_row, zero_row))

    def write(index, _):
        at = pl.ds(pl.multiple_of(index * b, b), b)
        out[0, index] = sol[at, 0:b]
        out[1, index] = sol[at, b:2 * b]
        return 0

    lax.fori_loop(0, 9, write, 0)

    for t in (0, 1):
        for copies in (gy_early[t], gy_late[t]):
            @pl.when(gy_to[t])
            def _(copies=copies):
                for copy in copies:
                    copy.wait_send()
    for s in (0, 1):
        @pl.when(gx_to[s])
        def _(s=s):
            for copy in gx_direct[s]:
                copy.wait_send()
        for t in (0, 1):
            @pl.when(jnp.logical_and(gy_from[t], gx_to[s]))
            def _(s=s, t=t):
                for copy in diag[s, t]:
                    copy.wait_send()


def entry(*refs):
    blocks, masks, rhs, limits, own_masks, out, *scratch = refs
    kernel(blocks, masks, rhs, (limits, own_masks), out, *scratch)


def shards(blocks, pair_mask, rhs_rows, counts):
    groups = blocks.shape[0]
    b = blocks.shape[-1]
    atoms = pair_mask.shape[-1]
    orb = b // atoms
    blocks = blocks.reshape(groups, 3, 3, b, b)
    rhs = rhs_rows.reshape(groups, 3, 3, b, b)
    masks = jnp.repeat(pair_mask.astype(F32), orb, axis=-1).reshape(groups, 3, 3, atoms, b)
    limits = jnp.repeat(counts.astype(F32), orb, axis=-1).reshape(1, groups * b)
    field = pltpu.VMEM((9 * b, 2 * b), F32)
    any_spec = pl.BlockSpec(memory_space=pl.ANY)
    vmem_spec = pl.BlockSpec(memory_space=pltpu.VMEM)
    copies = 2 * 11 + 2 * 3 + 4 * 3
    solved = pl.pallas_call(
        entry,
        out_shape=jax.ShapeDtypeStruct((groups, 9, b, b), F32),
        in_specs=[any_spec, any_spec, any_spec, vmem_spec, vmem_spec],
        out_specs=vmem_spec,
        scratch_shapes=[
            pltpu.VMEM((groups, 3, 3, b, b), F32),
            pltpu.VMEM((2, groups, 3, 2, b, b), F32),
            pltpu.VMEM((2, 2, 3, b, b), F32),
            pltpu.VMEM((2, 2, 2, 2, b, b), F32),
            pltpu.VMEM((2, groups, 3, 2, atoms, b), F32),
            pltpu.VMEM((2, 2, 3, atoms, b), F32),
            pltpu.VMEM((2, 2, 2, 2, atoms, b), F32),
            pltpu.VMEM((2, 2, b, b), F32),
            pltpu.VMEM((2, 2, 3 * b, 9 * b), BF16),
            pltpu.VMEM((2, 2, 3 * b, 6 * b), BF16),
            pltpu.VMEM((12 * b, 2 * b), BF16),
            pltpu.VMEM((12 * b, 2 * b), BF16),
            field, field, field, field, field, field, field, field, field, field,
            pltpu.SemaphoreType.DMA((copies,)),
            pltpu.SemaphoreType.DMA((copies,)),
            pltpu.SemaphoreType.DMA((5,)),
        ],
        compiler_params=pltpu.CompilerParams(
            collective_id=0, has_side_effects=True, vmem_limit_bytes=60 * 1024 * 1024
        ),
    )(blocks, masks, rhs, limits, masks)
    return solved.reshape(groups, 1, 9, b, b)


def solution(mesh):
    spec = P("gx", "gy", None, None, None)
    return jax.shard_map(
        shards,
        mesh=mesh,
        in_specs=(spec, spec, spec, P("gx", "gy", None)),
        out_specs=spec,
        check_vma=False,
    )
```

```python
import functools

import jax
import jax.numpy as jnp
from jax import lax
from jax.experimental import pallas as pl
from jax.experimental.pallas import tpu as pltpu
from jax.sharding import PartitionSpec as P

ITERS = 3
MESH = pl.DeviceIdType.MESH
F32 = jnp.float32
BF16 = jnp.bfloat16
CHUNK = 64


def guarded(top, bottom, floor_val):
    return top * bottom / (bottom * bottom + floor_val * floor_val)


def split(value):
    high = value.astype(BF16)
    return high, (value - high.astype(F32)).astype(BF16)


def kernel(
    blocks, masks, rhs, limits, own_masks, out,
    own_c, gy_c, gx_c, dg_c, gy_m, gx_m, dg_m, gy_r,
    mid, edge, v_hi, v_lo, res,
    shadow, w_vec, y_first, y_second, u_first, u_second, vec, direc, sol,
    send_sem, recv_sem, local_sem,
):
    b = blocks.shape[-1]
    atoms = masks.shape[-1]
    orb = b // atoms
    strip = 3 * b
    rows = 9 * b
    gx, gy = lax.axis_index("gx"), lax.axis_index("gy")
    ngx, ngy = lax.axis_size("gx"), lax.axis_size("gy")
    gx_to = (gx < ngx - 1, gx > 0)
    gx_from = (gx > 0, gx < ngx - 1)
    gy_to = (gy < ngy - 1, gy > 0)
    gy_from = (gy > 0, gy < ngy - 1)
    gx_dev = ((gx + 1, gy), (gx - 1, gy))
    gy_dev = ((gx, gy + 1), (gx, gy - 1))

    def place(ref, group, row_off, col_off):
        return ref.at[
            pl.ds(strip * (row_off + 1) + b * (col_off + 1), b), pl.ds(b * group, b)
        ]

    count = [0]

    def remote(src, dst, device):
        number = count[0]
        count[0] += 1
        return pltpu.make_async_remote_copy(
            src_ref=src, dst_ref=dst, send_sem=send_sem.at[number],
            recv_sem=recv_sem.at[number], device_id=device, device_id_type=MESH,
        )

    row_of = (1, 0)
    ou_of = (1, 0)
    ov_of = (1, 0)
    far = (2, 0)
    pairs = ((0, 0, 1, 0), (0, 1, 2, -1), (1, 0, 0, 1), (1, 1, 1, 0))

    gy_early, gy_rhs, gy_late, gx_direct, diag = {}, {}, {}, {}, {}
    for t in (0, 1):
        early, right, late = [], [], []
        ov = far[t]
        early.append(remote(
            masks.at[:, :, pl.ds(ov_of[t], 2)], gy_m.at[t], gy_dev[t]))
        for s in (0, 1):
            early.append(remote(
                rhs.at[row_of[s], far[s], ov], gy_r.at[t, s], gy_dev[t]))
        for s in (0, 1):
            early.append(remote(
                blocks.at[row_of[s], pl.ds(ou_of[s], 2), pl.ds(ov_of[t], 2)],
                gy_c.at[t, row_of[s], pl.ds(ou_of[s], 2)], gy_dev[t]))
        for row, group, ou, row_off in pairs:
            right.append(remote(
                rhs.at[row, ou, ov], place(shadow, group, row_off, 2 * t - 1), gy_dev[t]))
        for s in (0, 1):
            ou = 2 - far[s]
            late.append(remote(
                blocks.at[row_of[s], ou, pl.ds(ov_of[t], 2)],
                gy_c.at[t, row_of[s], ou], gy_dev[t]))
        gy_early[t], gy_rhs[t], gy_late[t] = early, right, late
    for s in (0, 1):
        row_off = 2 * s - 1
        gx_direct[s] = [
            remote(rhs.at[row_of[s], far[s], 1], place(shadow, s, row_off, 0), gx_dev[s]),
            remote(masks.at[row_of[s], pl.ds(ou_of[s], 2)], gx_m.at[s], gx_dev[s]),
            remote(blocks.at[row_of[s], pl.ds(ou_of[s], 2)], gx_c.at[s], gx_dev[s]),
        ]
        for t in (0, 1):
            diag[s, t] = [
                remote(gy_r.at[t, s], place(shadow, s, row_off, 2 * t - 1), gx_dev[s]),
                remote(gy_m.at[t, row_of[s], pl.ds(ou_of[s], 2)], dg_m.at[s, t], gx_dev[s]),
                remote(gy_c.at[t, row_of[s], pl.ds(ou_of[s], 2)], dg_c.at[s, t], gx_dev[s]),
            ]

    barrier = pltpu.get_barrier_semaphore()
    total = jnp.int32(0)
    for exists, device in zip(gx_to + gy_to, gx_dev + gy_dev):
        total = total + exists.astype(jnp.int32)

        @pl.when(exists)
        def _(device=device):
            pl.semaphore_signal(barrier, inc=1, device_id=device, device_id_type=MESH)
    pl.semaphore_wait(barrier, total)

    def start(condition, copies):
        @pl.when(condition)
        def _():
            for copy in copies:
                copy.start()

    for t in (0, 1):
        start(gy_to[t], gy_early[t])
    for s in (0, 1):
        start(gx_to[s], gx_direct[s])

    def sent(condition, copies):
        @pl.when(condition)
        def _():
            for copy in copies:
                copy.wait_send()

    locals_ = [pltpu.make_async_copy(blocks, own_c, local_sem.at[0])]
    for number, (row, group, ou, row_off) in enumerate(pairs):
        locals_.append(pltpu.make_async_copy(
            rhs.at[row, ou, 1], place(shadow, group, row_off, 0), local_sem.at[1 + number]))
    for copy in locals_:
        copy.start()

    def clear(ref):
        ref[...] = jnp.zeros(ref.shape, ref.dtype)

    zero = jnp.zeros((b, b), BF16)
    for group in (0, 1):
        for part in (0, 1):
            for t in (0, 1):
                at = 2 * strip * (1 - group) + b * t
                mid[group, part, 2 * b * t:2 * b * t + b, at:at + 2 * b] = jnp.zeros(
                    (b, 2 * b), BF16)

    def clear_rows(ref):
        def body(index, _):
            ref[pl.ds(index * b, b), :] = jnp.zeros((b, ref.shape[1]), ref.dtype)
            return 0
        lax.fori_loop(0, ref.shape[0] // b, body, 0)

    for ref in (u_second, vec, direc, sol):
        clear_rows(ref)
    clear_rows(v_hi)
    clear_rows(v_lo)
    for ref in (mid, edge):
        for which in (0, 1):
            for part in (0, 1):
                for near in range(ref.shape[-1] // strip):
                    ref[which, part, 0:b, strip * near + 2 * b:strip * near + 3 * b] = zero
                    ref[which, part, 2 * b:3 * b, strip * near:strip * near + b] = zero

    spread = (
        lax.broadcasted_iota(jnp.int32, (atoms, b), 1) // orb
        == lax.broadcasted_iota(jnp.int32, (atoms, b), 0)
    ).astype(F32)

    def widen(value):
        flat = value.astype(F32).reshape(-1, atoms)
        wide = jnp.dot(flat, spread, preferred_element_type=F32)
        return wide.reshape(value.shape[:-1] + (b,))

    def put(w, c, ou, ov, value, mask):
        masked = (value.reshape(b // orb, orb, b) * mask[:, None, :]).reshape(b, b)
        high, low = split(masked)
        base = (0, 0, 1, 2)[w]
        ref, which = ((edge, 0), (mid, 0), (mid, 1), (edge, 1))[w]
        col = strip * (w + ou - 1 - base) + b * (c + ov - 1)
        ref[which, 0, b * c:b * (c + 1), col:col + b] = high
        ref[which, 1, b * c:b * (c + 1), col:col + b] = low

    def finish(condition, copies, otherwise):
        @pl.when(condition)
        def _():
            for copy in copies:
                copy.wait_recv()

        @pl.when(jnp.logical_not(condition))
        def _():
            for ref in otherwise:
                clear(ref)

    locals_[0].wait()
    own_m = widen(own_masks[...])
    for row in (0, 1):
        for ou in range(3):
            for ov in range(3):
                put(row + 1, 1, ou, ov, own_c[row, ou, ov], own_m[row, ou, ov])

    for t in (0, 1):
        sent(gy_to[t], gy_early[t])
        start(gy_to[t], gy_rhs[t])
    for s in (0, 1):
        for t in (0, 1):
            @pl.when(gy_from[t])
            def _(s=s, t=t):
                if s == 0:
                    gy_early[t][0].wait_recv()
                gy_early[t][1 + s].wait_recv()
                gy_early[t][3 + s].wait_recv()
            start(jnp.logical_and(gy_from[t], gx_to[s]), diag[s, t])
    for t in (0, 1):
        sent(gy_to[t], gy_rhs[t])
        start(gy_to[t], gy_late[t])

    for s in (0, 1):
        finish(gx_from[s], gx_direct[s],
               [place(shadow, s, 2 * s - 1, 0), gx_m.at[s], gx_c.at[s]])
        wide = widen(gx_m[s])
        for ou in range(2):
            for ov in range(3):
                put(3 * s, 1, ou + ou_of[s], ov, gx_c[s, ou, ov], wide[ou, ov])

    for t in (0, 1):
        @pl.when(jnp.logical_not(gy_from[t]))
        def _(t=t):
            clear(gy_m.at[t])
            for s in (0, 1):
                for ou in range(2):
                    for ov in range(2):
                        clear(gy_c.at[t, row_of[s], ou + ou_of[s], ov])
        gy_wide = widen(gy_m[t])
        for s in (0, 1):
            for ou in range(2):
                for ov in range(2):
                    at = (t, row_of[s], ou + ou_of[s], ov)
                    put(row_of[s] + 1, 2 * t, at[2], ov + ov_of[t], gy_c[at], gy_wide[at[1:]])
    for t in (0, 1):
        for s in (0, 1):
            finish(jnp.logical_and(gx_from[s], gy_from[t]), diag[s, t],
                   [place(shadow, s, 2 * s - 1, 2 * t - 1), dg_m.at[s, t], dg_c.at[s, t]])
            wide = widen(dg_m[s, t])
            for ou in range(2):
                for ov in range(2):
                    put(3 * s, 2 * t, ou + ou_of[s], ov + ov_of[t],
                        dg_c[s, t, ou, ov], wide[ou, ov])
    for copy in locals_[1:]:
        copy.wait()
    for t in (0, 1):
        finish(gy_from[t], gy_rhs[t],
               [place(shadow, group, row_off, 2 * t - 1) for _, group, _, row_off in pairs])
    def over_chunks(body, sums):
        def step(index, carry):
            return body(pl.ds(pl.multiple_of(index * CHUNK, CHUNK), CHUNK), index * CHUNK, carry)
        return lax.fori_loop(
            0, rows // CHUNK, step, tuple(jnp.zeros((8, 2 * b), F32) for _ in range(sums)))

    def fold(value):
        return jnp.sum(value.reshape(CHUNK // 8, 8, 2 * b), axis=0)

    def column(value):
        return jnp.sum(value, axis=0, keepdims=True)

    def store_split(first, value):
        high, low = split(value)
        for ref, part in ((v_hi, high), (v_lo, low)):
            ref[pl.ds(pl.multiple_of(first, CHUNK), CHUNK), 0:b] = part[:, 0:b]
            ref[pl.ds(pl.multiple_of(first + strip, CHUNK), CHUNK), b:2 * b] = part[:, b:]

    def product(left, right):
        return jnp.dot(left, right, preferred_element_type=F32)

    def apply():
        for w in range(4):
            if w in (0, 3):
                which = w // 3
                near = pl.ds(2 * strip * which, 2 * strip)
                cols = slice(b * which, b * (which + 1))
                high, low = edge[which, 0], edge[which, 1]
            else:
                near = pl.ds(strip * (w - 1), 3 * strip)
                cols = slice(0, 2 * b)
                high, low = mid[w - 1, 0], mid[w - 1, 1]
            v_high, v_low = v_hi[near, cols], v_lo[near, cols]
            value = product(high, v_high) + product(low, v_high) + product(high, v_low)
            if w < 3:
                res[strip * w:strip * (w + 1), 0:b] = value[:, 0:b]
            if w > 0:
                res[strip * (w - 1):strip * w, b:2 * b] = value[:, -b:]

    def prepare(at, first, sums):
        value = shadow[at, :]
        w_vec[at, :] = value
        y_first[at, :] = value
        store_split(first, value)
        return (sums[0] + fold(value * value),)

    norm = column(over_chunks(prepare, 1)[0])
    limit = jnp.concatenate(
        [widen(jnp.broadcast_to(limits[group], (atoms, atoms)))[0:1] for group in (0, 1)], axis=1)
    apply()
    for t in (0, 1):
        finish(gy_from[t], gy_late[t],
               [gy_c.at[t, row_of[s], 2 - far[s]] for s in (0, 1)])
        gy_wide = widen(gy_m[t])
        for s in (0, 1):
            for ov in range(2):
                at = (t, row_of[s], 2 - far[s], ov)
                put(row_of[s] + 1, 2 * t, at[2], ov + ov_of[t], gy_c[at], gy_wide[at[1:]])
    for group in (0, 1):
        for t in (0, 1):
            here = pl.ds(b * 2 * t, b)
            cols = pl.ds(2 * strip * (1 - group) + b * t, 2 * b)
            source = pl.ds(strip * (2 - group) + b * t, 2 * b)
            v_high, v_low = v_hi[source, :], v_lo[source, :]
            high, low = mid[group, 0, here, cols], mid[group, 1, here, cols]
            value = product(high, v_high) + product(low, v_high) + product(high, v_low)
            for k in (0, 1):
                into, lanes = pl.ds(strip * (group + 1 - k) + b * 2 * t, b), pl.ds(b * k, b)
                res[into, lanes] = res[into, lanes] + value[:, b * k:b * (k + 1)]

    def iteration(index, carry):
        rho, beta, tau, theta, eta, ratio = carry
        active = (limit > index.astype(F32)).astype(F32)

        @pl.when(index > 0)
        def _():
            apply()

        def after_first(at, first, sums):
            image = y_first[at, :] - res[at, :]
            u_first[at, :] = image
            value = image + beta * (u_second[at, :] + beta * vec[at, :])
            vec[at, :] = value
            return sums[0] + fold(value * value), sums[1] + fold(shadow[at, :] * value)

        square, along = (column(v) for v in over_chunks(after_first, 2))
        alpha = guarded(rho, along, 0.1 * jnp.sqrt(norm * (square + 1e-06)))
        ratio = guarded(1.0, alpha, 0.1)
        keep = theta * theta * eta * ratio

        def between(at, first, sums):
            y_one = y_first[at, :]
            residual = w_vec[at, :] - alpha * u_first[at, :]
            w_vec[at, :] = residual
            direc[at, :] = y_one + keep * direc[at, :]
            second = y_one - alpha * vec[at, :]
            y_second[at, :] = second
            store_split(first, second)
            return (sums[0] + fold(residual * residual),)

        size = column(over_chunks(between, 1)[0])

        def turn(size, tau):
            theta = jnp.sqrt(size) / tau
            cosine = 1.0 / jnp.sqrt(1.0 + theta * theta)
            return theta, tau * theta * cosine, cosine * cosine * alpha

        theta, tau, eta = turn(size, tau)
        eta_one = active * eta
        apply()

        def after_second(at, first, sums):
            image = y_second[at, :] - res[at, :]
            u_second[at, :] = image
            residual = w_vec[at, :] - alpha * image
            w_vec[at, :] = residual
            return sums[0] + fold(residual * residual), sums[1] + fold(shadow[at, :] * residual)

        size, rho_next = (column(v) for v in over_chunks(after_second, 2))
        keep = theta * theta * eta * ratio
        theta, tau, eta = turn(size, tau)
        eta_two = active * eta
        return keep, eta_one, eta_two, rho_next, size, tau, theta, eta, ratio

    def close(beta, keep, eta_one, eta_two):
        def body(at, first, sums):
            one, second = direc[at, :], y_second[at, :]
            two = second + keep * one
            direc[at, :] = two
            sol[at, :] = sol[at, :] + eta_one * one + eta_two * two
            value = w_vec[at, :] + beta * second
            y_first[at, :] = value
            store_split(first, value)
            return sums
        over_chunks(body, 0)

    zero_row = jnp.zeros_like(norm)

    def whole(index, carry):
        rho, floor, beta, tau, theta, eta, ratio = carry
        keep, eta_one, eta_two, rho_next, size, tau, theta, eta, ratio = iteration(
            index, (rho, beta, tau, theta, eta, ratio))
        beta = guarded(rho_next, rho, floor)
        floor = 0.1 * jnp.sqrt(norm * size)
        close(beta, keep, eta_one, eta_two)
        return rho_next, floor, beta, tau, theta, eta, ratio

    lax.fori_loop(0, ITERS, whole, (
        norm, 0.1 * norm, zero_row, jnp.sqrt(norm), zero_row, zero_row, zero_row))

    def write(index, _):
        at = pl.ds(pl.multiple_of(index * b, b), b)
        out[0, index] = sol[at, 0:b]
        out[1, index] = sol[at, b:2 * b]
        return 0

    lax.fori_loop(0, 9, write, 0)

    for t in (0, 1):
        sent(gy_to[t], gy_late[t])
    for s in (0, 1):
        sent(gx_to[s], gx_direct[s])
        for t in (0, 1):
            sent(jnp.logical_and(gy_from[t], gx_to[s]), diag[s, t])


def shards(blocks, pair_mask, rhs_rows, counts):
    groups = blocks.shape[0]
    b = blocks.shape[-1]
    atoms = pair_mask.shape[-1]
    blocks = blocks.reshape(groups, 3, 3, b, b)
    rhs = rhs_rows.reshape(groups, 3, 3, b, b)
    masks = pair_mask.reshape(groups, 3, 3, atoms, atoms)
    field = pltpu.VMEM((9 * b, 2 * b), F32)
    any_spec = pl.BlockSpec(memory_space=pl.ANY)
    vmem_spec = pl.BlockSpec(memory_space=pltpu.VMEM)
    copies = 2 * 11 + 2 * 3 + 4 * 3
    solved = pl.pallas_call(
        kernel,
        out_shape=pltpu.VMEM((groups, 9, b, b), F32),
        in_specs=[any_spec, any_spec, any_spec, vmem_spec, vmem_spec],
        out_specs=vmem_spec,
        scratch_shapes=[
            pltpu.VMEM((groups, 3, 3, b, b), F32),
            pltpu.VMEM((2, groups, 3, 2, b, b), F32),
            pltpu.VMEM((2, 2, 3, b, b), F32),
            pltpu.VMEM((2, 2, 2, 2, b, b), F32),
            pltpu.VMEM((2, groups, 3, 2, atoms, atoms), jnp.int32),
            pltpu.VMEM((2, 2, 3, atoms, atoms), jnp.int32),
            pltpu.VMEM((2, 2, 2, 2, atoms, atoms), jnp.int32),
            pltpu.VMEM((2, 2, b, b), F32),
            pltpu.VMEM((2, 2, 3 * b, 9 * b), BF16),
            pltpu.VMEM((2, 2, 3 * b, 6 * b), BF16),
            pltpu.VMEM((12 * b, 2 * b), BF16),
            pltpu.VMEM((12 * b, 2 * b), BF16),
            field, field, field, field, field, field, field, field, field, field,
            pltpu.SemaphoreType.DMA((copies,)),
            pltpu.SemaphoreType.DMA((copies,)),
            pltpu.SemaphoreType.DMA((5,)),
        ],
        compiler_params=pltpu.CompilerParams(
            collective_id=0, has_side_effects=True, vmem_limit_bytes=60 * 1024 * 1024
        ),
    )(blocks, masks, rhs, counts, masks)
    return solved.reshape(groups, 1, 9, b, b)


def solution(mesh):
    spec = P("gx", "gy", None, None, None)
    return jax.shard_map(
        shards,
        mesh=mesh,
        in_specs=(spec, spec, spec, P("gx", "gy", None)),
        out_specs=spec,
        check_vma=False,
    )
```
